32 devices in a mesh: row: 4 (over z), col: 8 (over y, x, core).
Axes of the slice: x: 2, y: 2, z: 4, core: 2. Of those that a mesh axis runs over, the one named last changes fastest.
Arguments:
- region: float32 [8, 1024, 8, 1024], P(None, 'col', None, 'row'), may hold values from -6 to 6
- l_panels: bfloat16 [3, 1024, 11, 1024], P(None, 'col', None, 'row'), may hold values from -0.0625 to 0.0625
- u_panels: bfloat16 [3, 11, 1024, 1024], P(None, None, 'col', 'row'), may hold values from -0.0625 to 0.0625
- diag_inv: float32 [3, 1024, 1024], P(None, 'col', 'row'), may hold values from -6 to 6
- pattern: int32 [3, 11, 8], replicated, may hold values from 0 to 1, as said below
Outputs:
- inverse: float32 [11, 1024, 11, 1024], P(None, 'col', None, 'row')
The draws below stay inside these ranges and needn't reach their ends.
Inputs may be any that keep to these rules, and one draw needn't show every extreme that they name: pattern[s] marks the 128-row blocks in the structure of supernode s: only blocks of segments after s; for the last supernode only blocks of the ancestor region; for every other supernode all blocks of one later supernode (its parent in the elimination tree) and otherwise only blocks that the parent's pattern also marks.
All inputs are finite; a program needn't handle non-finite values.
Results may differ from the reference program's by a relative error of at most 0.0003.
Values may be sent and summed in bfloat16 or wider, within the bound.
A program may use at most 128 MiB of HBM per device.

```python
import jax
import jax.numpy as jnp
from jax import lax

W = 1024
BLK = 128
NSUP = 3
ASEG = 8
NSEG = 11
WB = 8


def draw_pattern(key, part):
    seg_index = jnp.arange(NSEG, dtype=jnp.int32)[:, None] * jnp.ones((1, WB), jnp.int32)
    structs = jnp.zeros((NSUP, NSEG, WB), jnp.int32)
    region_bits = jax.random.randint(jax.random.fold_in(key, 7), (NSEG, WB), 0, 2)
    structs = structs.at[NSUP - 1].set(region_bits * (seg_index >= NSUP).astype(jnp.int32))
    for level in range(NSUP - 2, -1, -1):
        parent = jax.random.randint(jax.random.fold_in(key, 100 + level), (), level + 1, NSUP)
        kept_bits = (jax.random.randint(jax.random.fold_in(key, 200 + level), (NSEG, WB), 0, 4) > 0).astype(jnp.int32)
        parent_blocks = (seg_index == parent).astype(jnp.int32)
        structs = structs.at[level].set(jnp.maximum(parent_blocks, structs[parent] * kept_bits))
    return structs


def steps_of(stream_key, shape, cuts, smallest, top_value):
    def one(position, parts):
        heights = jax.random.uniform(jax.random.fold_in(jax.random.fold_in(stream_key, 6), position), (parts,), jnp.float32, smallest / len(cuts), top_value / len(cuts))
        return jnp.repeat(jnp.exp(heights), shape[position] // parts).reshape((-1,) + (1,) * (len(shape) - position - 1))

    gain = one(*cuts[0])
    for cut in cuts[1:]:
        gain = gain * one(*cut)
    return gain


def bell_draw(stream_key, shape, width, bound, shards=(), kind=jnp.bfloat16):
    loudness = steps_of(stream_key, shape, shards, -0.22, 0.18) if shards else 1.0
    entries = jax.random.normal(stream_key, shape, jnp.float32) * width * loudness
    return jnp.minimum(jnp.maximum(entries, -bound), bound).astype(kind)


def setup_inputs(seed: int = 0) -> dict:
    streams_of = jax.random.split(jax.random.key(seed), 6)
    return {
        "region": bell_draw(streams_of[0], (ASEG, W, ASEG, W), 1.0, 6.0, ((1, 8), (3, 4)), jnp.float32),
        "l_panels": bell_draw(streams_of[1], (NSUP, W, NSEG, W), (ASEG * W) ** -0.5, 0.0625, ((1, 8), (3, 4))),
        "u_panels": bell_draw(streams_of[2], (NSUP, NSEG, W, W), (ASEG * W) ** -0.5, 0.0625, ((2, 8), (3, 4))),
        "diag_inv": bell_draw(streams_of[3], (NSUP, W, W), 1.0, 6.0, ((1, 8), (2, 4)), jnp.float32),
        "pattern": draw_pattern(jax.random.fold_in(streams_of[5], 71), 0),
    }


def reference(region, l_panels, u_panels, diag_inv, pattern):
    inverse = jnp.zeros((NSEG, W, NSEG, W), jnp.float32)
    inverse = inverse.at[NSUP:, :, NSUP:, :].set(region.astype(jnp.float32))
    block_mask = jnp.repeat(pattern.astype(jnp.float32), BLK, axis=2)
    for level in reversed(range(NSUP)):
        mask_now = block_mask[level]
        lower = l_panels[level].astype(jnp.float32) * mask_now[None, :, :]
        upper = u_panels[level].astype(jnp.float32) * mask_now[:, :, None]
        column = -mask_now[:, :, None] * jnp.einsum("ajbk,wbk->ajw", inverse, lower, precision=lax.Precision.HIGHEST)
        row_panel = -mask_now[None, :, :] * jnp.einsum("akw,akbj->wbj", upper, inverse, precision=lax.Precision.HIGHEST)
        diagonal = diag_inv[level] - jnp.einsum("akw,akv->wv", upper, column, precision=lax.Precision.HIGHEST)
        inverse = inverse.at[:, :, level, :].set(column)
        inverse = inverse.at[level].set(row_panel)
        inverse = inverse.at[level, :, level, :].set(diagonal)
    return inverse
```

```python
import jax
import jax.numpy as jnp
from jax import lax
from jax.sharding import PartitionSpec as P

BLK = 128
NSUP = 3
NSEG = 11


def split(x):
    hi = lax.reduce_precision(x, 8, 7)
    return hi.astype(jnp.bfloat16), (x - hi).astype(jnp.bfloat16)


def two_pass(spec, first, second, wide_first):
    out = None
    for part in first if wide_first else second:
        args = (part, second) if wide_first else (first, part)
        term = jnp.einsum(spec, *args, preferred_element_type=jnp.float32)
        out = term if out is None else out + term
    return out


def scatter_sum(terms, axis, n):
    parts = terms.reshape((n, terms.shape[0] // n) + terms.shape[1:])
    return jnp.sum(lax.all_to_all(parts, axis, 0, 0), axis=0)


def per_device(n_col, region, l_panels, u_panels, diag_inv, pattern):
    rows_here = region.shape[1]
    cols_here = region.shape[3]
    row_index = lax.axis_index("row")
    col_index = lax.axis_index("col")
    block_mask = jnp.repeat(pattern.astype(jnp.float32), BLK, axis=2)
    mask_rows = lax.dynamic_slice_in_dim(block_mask, col_index * rows_here, rows_here, 2)
    mask_cols = lax.dynamic_slice_in_dim(block_mask, row_index * cols_here, cols_here, 2)
    inverse = jnp.zeros((NSEG, rows_here, NSEG, cols_here), jnp.float32)
    inverse = inverse.at[NSUP:, :, NSUP:, :].set(region)
    lowers, uppers = {}, {}
    for level in reversed(range(NSUP)):
        start = level + 1
        lower = l_panels[level][:, start:, :] * mask_cols[level, None, start:, :].astype(jnp.bfloat16)
        upper = u_panels[level][start:] * mask_rows[level, start:, :, None].astype(jnp.bfloat16)
        lowers[level] = lax.all_gather(lower, "col", axis=0, tiled=True)
        uppers[level] = lax.all_gather(upper, "row", axis=2, tiled=True)
    for level in reversed(range(NSUP)):
        start = level + 1
        lower, upper = lowers[level], uppers[level]
        known = split(inverse[start:, :, start:, :])
        col_terms = two_pass("ajbk,wbk->ajw", known, lower, True)
        col_sum = lax.psum_scatter(col_terms, "row", scatter_dimension=2, tiled=True)
        row_terms = two_pass("akw,akbj->wbj", upper, known, False)
        row_sum = scatter_sum(row_terms, "col", n_col)
        row_panel = -mask_cols[level, None, start:, :] * row_sum
        column = -mask_rows[level, start:, :, None] * col_sum
        diag_terms = two_pass("akw,akv->wv", upper, split(column), False)
        diagonal = diag_inv[level] - scatter_sum(diag_terms, "col", n_col)
        inverse = inverse.at[start:, :, level, :].set(column)
        inverse = inverse.at[level, :, start:, :].set(row_panel)
        inverse = inverse.at[level, :, level, :].set(diagonal)
    return inverse


def solution(mesh):
    in_specs = (
        P(None, "col", None, "row"),
        P(None, "col", None, "row"),
        P(None, None, "col", "row"),
        P(None, "col", "row"),
        P(),
    )
    out_specs = P(None, "col", None, "row")
    n_col = mesh.shape["col"]

    def body(*args):
        return per_device(n_col, *args)

    return jax.shard_map(
        body, mesh=mesh, in_specs=in_specs, out_specs=out_specs, check_vma=False
    )
```
